256 devices in a mesh: dp: 32 (over x, z_lo, y), tensor: 8 (over z_hi, core).
Axes of the slice: x: 4, y: 4, z: 8 (z_hi: 4, z_lo: 2; z = z_hi * 2 + z_lo), core: 2. Of those that a mesh axis runs over, the one named last changes fastest.
Arguments:
- gradient: bfloat16 [2, 2048, 16384], P(None, 'dp', 'tensor'), may hold values from -1000 to 1000
- master: float32 [2, 2048, 16384], P(None, 'dp', 'tensor'), may hold values from -0.046875 to 0.046875
- first_moment: float32 [2, 2048, 16384], P(None, 'dp', 'tensor'), may hold values from -3 to 3
- second_moment: float32 [2, 2048, 16384], P(None, 'dp', 'tensor'), may hold values from 0.05 to 1
- residual: bfloat16 [8192, 16384], P('dp', 'tensor'), may hold values from -1500 to 1500
- norm_gain: float32 [16384], replicated, may hold values from 0.5 to 2
- queries: bfloat16 [8192, 128, 128], P('dp', 'tensor'), may hold values from -170 to 170
- layer_cache: bfloat16 [8192, 2, 8, 32, 128], P('dp', None, 'tensor'), may hold values from -4.5 to 4.5
- fresh_entries: bfloat16 [8192, 2, 8, 128], P('dp', None, 'tensor'), may hold values from -6 to 6
- lengths: int32 [8192], P('dp'), may hold values from 2 to 32, as said below
- shard_table: int32 [32], replicated, may hold values from 0 to 31, each once
Outputs:
- new_first: float32 [2, 2048, 16384], P(None, 'dp', 'tensor')
- new_second: float32 [2, 2048, 16384], P(None, 'dp', 'tensor')
- attended: bfloat16 [8192, 128, 128], P('dp', 'tensor')
- activated: bfloat16 [8192, 2048], P('dp', 'tensor')
The draws below stay inside these ranges and needn't reach their ends.
Inputs may be any that keep to these rules, and one draw needn't show every extreme that they name: `lengths`: every row has 2 or more valid positions, and in each rollout group's rows one row has all 32. `shard_table`: A permutation of the learner shards.
All inputs are finite; a program needn't handle non-finite values.
Results may differ from the reference program's by a relative error of at most 0.0072.
Values may be sent and summed in bfloat16 or wider, within the bound.
A program may use at most 128 MiB of HBM per device.

```python
import math
import jax
import jax.numpy as jnp
from jax import lax

D = 16384
HQ = 128
KVH = 8
HD = 128
UNITS_DEV = 8
ROWS_DEV = 256
CACHE = 32
ROWS = 8192
SLAB = 2048
N_DP = 32
N_TENSOR = 8


def spread_scales(key, count):
    return 10.0 ** jax.random.uniform(key, (count,), jnp.float32)


def draw_gradient(key, part):
    base_key, column_key = jax.random.split(jax.random.fold_in(key, 1), 2)
    loud_key = jax.random.fold_in(key, 21)
    rising = 10.0 ** (jnp.arange(SLAB, dtype=jnp.float32) / SLAB)
    columns = spread_scales(column_key, D)
    loudness = 10.0 ** jax.random.uniform(loud_key, (N_DP, N_TENSOR), jnp.float32, -1.0, 0.0)
    entries = jnp.clip(jax.random.normal(base_key, (2, SLAB, D), jnp.float32), -6.0, 6.0)
    entries = entries * rising[None, :, None] * columns[None, None, :]
    blocked = entries.reshape(2, N_DP, SLAB // N_DP, N_TENSOR, D // N_TENSOR)
    blocked = blocked * loudness[None, :, None, :, None]
    return blocked.reshape(2, SLAB, D).astype(jnp.bfloat16)


def draw_residual(key, part):
    base_key, row_key, column_key = jax.random.split(jax.random.fold_in(key, 2), 3)
    row_scales = spread_scales(row_key, ROWS)
    columns = spread_scales(column_key, D)
    entries = jnp.clip(jax.random.normal(base_key, (ROWS, D), jnp.float32), -6.0, 6.0)
    return (entries * row_scales[:, None] * columns[None, :]).astype(jnp.bfloat16)


def draw_layer_cache(key, part):
    entries = jnp.clip(jax.random.normal(jax.random.fold_in(key, 3), (ROWS, 2, KVH, CACHE, HD), jnp.float32), -4.5, 4.5)
    return entries.astype(jnp.bfloat16)


def draw_queries(key, part):
    entries = jnp.clip(jax.random.normal(jax.random.fold_in(key, 5), (ROWS, HQ, HD), jnp.float32), -4.5, 4.5)
    return entries.astype(jnp.bfloat16)


def draw_lengths(key, part):
    drawn_lengths = jax.random.randint(jax.random.fold_in(key, 4), (ROWS,), 2, CACHE + 1)
    full_rows = jnp.arange(ROWS) % ROWS_DEV == 0
    return jnp.where(full_rows, CACHE, drawn_lengths).astype(jnp.int32)


def block_levels(key, shape, shards, smallest, largest):
    factor_of, own = 1.0, jax.random.fold_in(key, 6)
    for position, shards_of in shards:
        heights = jnp.exp(jax.random.uniform(jax.random.fold_in(own, position), (shards_of,), jnp.float32, smallest / len(shards), largest / len(shards)))
        factor_of = factor_of * jnp.repeat(heights, shape[position] // shards_of).reshape([-1 if axis == position else 1 for axis in range(len(shape))])
    return factor_of


def scatter_about(key, dims, scale, most, pieces=(), kind=jnp.bfloat16):
    values = jax.random.normal(key, dims, jnp.float32) * scale
    if len(pieces) > 0:
        values = block_levels(key, dims, pieces, -0.22, 0.18) * values
    return jnp.clip(values, min=-most, max=most).astype(kind)


def setup_inputs(seed: int = 0) -> dict:
    streams_of = jax.random.split(jax.random.key(seed), 12)
    gradient = draw_gradient(jax.random.fold_in(streams_of[11], 71), 0)
    master = scatter_about(streams_of[1], (2, SLAB, D), D ** -0.5, 0.046875, ((1, 32), (2, 8)), jnp.float32)
    first_moment = scatter_about(streams_of[2], (2, SLAB, D), 0.5, 3.0, ((1, 32), (2, 8)), jnp.float32)
    second_moment = jnp.clip(jnp.exp(math.log(1.0) - 2.9957323 * jax.random.uniform(streams_of[3], (2, SLAB, D), jnp.float32) ** block_levels(streams_of[3], (2, SLAB, D), ((1, 32), (2, 8)), -0.2, 0.2)), 0.05, 1.0)
    residual = draw_residual(jax.random.fold_in(streams_of[11], 71), 0)
    norm_gain = jnp.clip(jnp.exp(jax.random.uniform(streams_of[5], (D,), jnp.float32, math.log(0.5), math.log(2.0))), 0.5, 2.0)
    queries = draw_queries(jax.random.fold_in(streams_of[11], 71), 0)
    layer_cache = draw_layer_cache(jax.random.fold_in(streams_of[11], 71), 0)
    fresh_entries = scatter_about(streams_of[8], (ROWS, 2, KVH, HD), 1.0, 6.0, ((0, 32), (2, 8)))
    lengths = draw_lengths(jax.random.fold_in(streams_of[11], 71), 0)
    shard_table = jax.random.permutation(streams_of[10], N_DP).astype(jnp.int32)
    return dict(gradient=gradient, master=master, first_moment=first_moment, second_moment=second_moment, residual=residual, norm_gain=norm_gain, queries=queries, layer_cache=layer_cache, fresh_entries=fresh_entries, lengths=lengths, shard_table=shard_table)


LEARN_RATE = 0.001
CLIP_LEVEL = 0.5
CLIP_EPSILON = 1e-06
FIRST_DECAY = 0.9
SECOND_DECAY = 0.95
FIRST_CORRECTION = 1.0 - 0.9 ** 10
SECOND_CORRECTION = 1.0 - 0.95 ** 10
ADAM_EPSILON = 1e-08
NORM_EPSILON = 1e-05

def attend(queries, layer_cache, fresh_entries, lengths):
    row_count, head_count, head_width = queries.shape
    group_count = layer_cache.shape[2]
    per_group = head_count // group_count
    score_scale = 1.0 / math.sqrt(head_width)
    grouped = queries.reshape(row_count, group_count, per_group, head_width).astype(jnp.float32)
    cached_keys = layer_cache[:, 0].astype(jnp.float32)
    cached_values = layer_cache[:, 1].astype(jnp.float32)
    scores = jnp.einsum('rghd,rgpd->rghp', grouped, cached_keys) * score_scale
    own_score = jnp.einsum('rghd,rgd->rgh', grouped, fresh_entries[:, 0].astype(jnp.float32)) * score_scale
    positions = lax.broadcasted_iota(jnp.int32, (row_count, 1, 1, cached_keys.shape[2]), 3)
    in_range = positions < lengths.astype(jnp.int32)[:, None, None, None]
    scores = jnp.where(in_range, scores, -jnp.inf)
    row_peak = jnp.maximum(lax.optimization_barrier(jnp.max(scores, axis=3)), own_score)
    cached_exp = jnp.exp(scores - row_peak[..., None])
    own_exp = jnp.exp(own_score - row_peak)
    denominator = lax.optimization_barrier(jnp.sum(cached_exp, axis=3)) + own_exp
    cached_prob = (cached_exp / denominator[..., None]).astype(jnp.bfloat16).astype(jnp.float32)
    own_prob = (own_exp / denominator).astype(jnp.bfloat16).astype(jnp.float32)
    combined = jnp.einsum('rghp,rgpd->rghd', cached_prob, cached_values)
    combined = combined + own_prob[..., None] * fresh_entries[:, 1].astype(jnp.float32)[:, :, None, :]
    return combined.reshape(row_count, head_count, head_width).astype(jnp.bfloat16)

def reference(gradient, master, first_moment, second_moment, residual, norm_gain, queries, layer_cache, fresh_entries, lengths, shard_table):
    gradient_wide = gradient.astype(jnp.float32)
    total_sum = jnp.sum(gradient_wide * gradient_wide)
    clip_limit = CLIP_LEVEL * math.sqrt(gradient.size)
    clip_factor = jnp.minimum(1.0, clip_limit / (jnp.sqrt(total_sum) + CLIP_EPSILON))
    clipped = gradient_wide * clip_factor
    new_first = FIRST_DECAY * first_moment + (1.0 - FIRST_DECAY) * clipped
    new_second = SECOND_DECAY * second_moment + (1.0 - SECOND_DECAY) * clipped * clipped
    adam_step = new_first / FIRST_CORRECTION / (jnp.sqrt(new_second / SECOND_CORRECTION) + ADAM_EPSILON)
    fresh_weight = (master - LEARN_RATE * adam_step).astype(jnp.bfloat16)
    residual_wide = residual.astype(jnp.float32)
    mean_square = lax.optimization_barrier(jnp.mean(residual_wide * residual_wide, axis=1, keepdims=True))
    normed = (residual_wide * lax.rsqrt(mean_square + NORM_EPSILON) * norm_gain).astype(jnp.bfloat16)
    normed_wide = normed.astype(jnp.float32)
    gate_sum = jnp.dot(normed_wide, fresh_weight[0].astype(jnp.float32).T, precision=lax.Precision.HIGHEST)
    up_sum = jnp.dot(normed_wide, fresh_weight[1].astype(jnp.float32).T, precision=lax.Precision.HIGHEST)
    hidden = jax.nn.silu(gate_sum) * up_sum
    blocks = hidden.reshape(ROWS, N_DP, N_TENSOR, UNITS_DEV)
    ordered = jnp.take(blocks, shard_table.astype(jnp.int32), axis=1)
    activated = jnp.transpose(ordered, (0, 2, 1, 3)).reshape(ROWS, SLAB).astype(jnp.bfloat16)

    def attend_block(block):
        return attend(block[0], block[1], block[2], block[3])
    attended = lax.map(attend_block, (queries.reshape(N_DP, ROWS_DEV, HQ, HD), layer_cache.reshape(N_DP, ROWS_DEV, 2, KVH, CACHE, HD), fresh_entries.reshape(N_DP, ROWS_DEV, 2, KVH, HD), lengths.reshape(N_DP, ROWS_DEV)))
    attended = attended.reshape(ROWS, HQ, HD)
    return (new_first, new_second, attended, activated)
```

```python
import math

import jax
import jax.numpy as jnp
from jax import lax
from jax.sharding import PartitionSpec as P

LEARN_RATE = 0.001
CLIP_LEVEL = 0.5
CLIP_EPSILON = 1e-06
FIRST_DECAY = 0.9
SECOND_DECAY = 0.95
FIRST_CORRECTION = 1.0 - 0.9**10
SECOND_CORRECTION = 1.0 - 0.95**10
ADAM_EPSILON = 1e-08
NORM_EPSILON = 1e-05
LINE = 4


def adam_update(gradient, master, first_moment, second_moment, total_sum, entry_count):
    clip_limit = CLIP_LEVEL * math.sqrt(entry_count)
    clip_factor = jnp.minimum(1.0, clip_limit / (jnp.sqrt(total_sum) + CLIP_EPSILON))
    clipped = gradient.astype(jnp.float32) * clip_factor
    new_first = FIRST_DECAY * first_moment + (1.0 - FIRST_DECAY) * clipped
    new_second = SECOND_DECAY * second_moment + (1.0 - SECOND_DECAY) * clipped * clipped
    adam_step = (
        new_first / FIRST_CORRECTION / (jnp.sqrt(new_second / SECOND_CORRECTION) + ADAM_EPSILON)
    )
    fresh_weight = (master - LEARN_RATE * adam_step).astype(jnp.bfloat16)
    return (new_first, new_second, fresh_weight)


def attend(queries, layer_cache, fresh_entries, lengths):
    row_count, head_count, head_width = queries.shape
    group_count = layer_cache.shape[2]
    per_group = head_count // group_count
    score_scale = 1.0 / math.sqrt(head_width)
    grouped = queries.reshape(row_count, group_count, per_group, head_width)
    cached_keys = layer_cache[:, 0]
    cached_values = layer_cache[:, 1]
    scores = (
        jnp.einsum("rghd,rgpd->rghp", grouped, cached_keys, preferred_element_type=jnp.float32)
        * score_scale
    )
    own_score = (
        jnp.einsum(
            "rghd,rgd->rgh", grouped, fresh_entries[:, 0], preferred_element_type=jnp.float32
        )
        * score_scale
    )
    positions = lax.broadcasted_iota(jnp.int32, (row_count, 1, 1, cached_keys.shape[2]), 3)
    in_range = positions < lengths[:, None, None, None]
    scores = jnp.where(in_range, scores, -jnp.inf)
    row_peak = jnp.maximum(jnp.max(scores, axis=3), own_score)
    cached_exp = jnp.exp(scores - row_peak[..., None])
    own_exp = jnp.exp(own_score - row_peak)
    denominator = jnp.sum(cached_exp, axis=3) + own_exp
    cached_prob = (cached_exp / denominator[..., None]).astype(jnp.bfloat16)
    own_prob = (own_exp / denominator).astype(jnp.bfloat16)
    combined = jnp.einsum(
        "rghp,rgpd->rghd", cached_prob, cached_values, preferred_element_type=jnp.float32
    )
    combined = (
        combined
        + own_prob[..., None].astype(jnp.float32)
        * fresh_entries[:, 1].astype(jnp.float32)[:, :, None, :]
    )
    return combined.reshape(row_count, head_count, head_width).astype(jnp.bfloat16)


def per_device(
    gradient,
    master,
    first_moment,
    second_moment,
    residual,
    norm_gain,
    queries,
    layer_cache,
    fresh_entries,
    lengths,
    shard_table,
):
    rows, width = residual.shape
    shards = lax.axis_size("dp")
    ranks = lax.axis_size("tensor")
    near = [[g * LINE + y for y in range(LINE)] for g in range(shards // LINE)]
    far = [[g * LINE + y for g in range(shards // LINE)] for y in range(LINE)]
    planes = shards // LINE

    wide = residual.astype(jnp.float32)
    row_sum = jnp.sum(wide * wide, axis=1)
    gradient_wide = gradient.astype(jnp.float32)
    grad_sum = jnp.sum(gradient_wide * gradient_wide)
    sums = lax.psum(jnp.concatenate([row_sum, jnp.broadcast_to(grad_sum, (rows,))]), "tensor")
    total_sum = lax.psum(sums[rows], "dp")
    row_sum, total_sum = lax.optimization_barrier((sums[:rows], total_sum))

    me = lax.axis_index("tensor")
    gain = lax.dynamic_slice_in_dim(norm_gain, me * width, width)
    scale = lax.rsqrt(row_sum / (width * ranks) + NORM_EPSILON)
    normed = (wide * scale[:, None] * gain).astype(jnp.bfloat16)
    normed = lax.all_gather(normed, "dp", axis=0, tiled=True, axis_index_groups=near)

    new_first, new_second, fresh_weight = adam_update(
        gradient, master, first_moment, second_moment, total_sum, gradient.size * shards * ranks
    )
    units = fresh_weight.shape[1] // ranks
    weights = lax.all_gather(fresh_weight, "dp", axis=0, axis_index_groups=far)
    flat = weights.reshape(planes * 2 * ranks * units, width)
    partial = lax.dot_general(
        flat, normed, (((1,), (1,)), ((), ())), preferred_element_type=jnp.float32
    ).astype(jnp.bfloat16)
    partial = partial.reshape(planes, 2, ranks, units, LINE * rows).transpose(2, 0, 1, 3, 4)
    partial = partial.reshape(ranks, planes * 2 * units, LINE * rows)
    summed = lax.psum_scatter(partial, "tensor", scatter_dimension=0, tiled=False)
    summed = summed.astype(jnp.float32).reshape(planes, 2, units, LINE * rows)
    hidden = (jax.nn.silu(summed[:, 0]) * summed[:, 1]).astype(jnp.bfloat16)
    hidden = hidden.reshape(planes * units, LINE * rows)
    hidden = lax.all_to_all(
        hidden, "dp", split_axis=1, concat_axis=0, tiled=True, axis_index_groups=near
    )
    hidden = hidden.reshape(LINE, planes, units, rows).transpose(1, 0, 2, 3)
    hidden = hidden.reshape(shards, units, rows)
    ordered = jnp.take(hidden, shard_table, axis=0)
    activated = ordered.reshape(shards * units, rows).T
    attended = attend(queries, layer_cache, fresh_entries, lengths)
    return (new_first, new_second, attended, activated)


def solution(mesh):
    return jax.shard_map(
        per_device,
        mesh=mesh,
        in_specs=(
            P(None, "dp", "tensor"),
            P(None, "dp", "tensor"),
            P(None, "dp", "tensor"),
            P(None, "dp", "tensor"),
            P("dp", "tensor"),
            P(),
            P("dp", "tensor", None),
            P("dp", None, "tensor", None, None),
            P("dp", None, "tensor", None),
            P("dp"),
            P(),
        ),
        out_specs=(
            P(None, "dp", "tensor"),
            P(None, "dp", "tensor"),
            P("dp", "tensor", None),
            P("dp", "tensor"),
        ),
        check_vma=False,
    )
```
